32 devices in a mesh: seq: 8 (over z, y), tensor: 4 (over x, core).
Axes of the slice: x: 2, y: 2, z: 4, core: 2. Of those that a mesh axis runs over, the one named last changes fastest.
Arguments:
- hidden_in: bfloat16 [1024, 8192], P('seq', 'tensor'), may hold values from -6 to 6
- grad_out: bfloat16 [1024, 8192], P('seq', 'tensor'), may hold values from -6 to 6
- slot_tokens: int32 [128], P('seq'), may hold values from 0 to 127, as said below
- live_counts: int32 [8], P('seq'), may hold values from 5 to 16, as said below
- norm_gain: float32 [8192], P('tensor'), may hold values from 0.5 to 1.5
- router_weight: float32 [8192], P('tensor'), may hold values from -0.0625 to 0.0625
- gate_weight: bfloat16 [8192, 24576], P('tensor', 'seq'), may hold values from -0.0625 to 0.0625
- up_weight: bfloat16 [8192, 24576], P('tensor', 'seq'), may hold values from -0.0625 to 0.0625
- down_weight: bfloat16 [24576, 8192], P('seq', 'tensor'), may hold values from -0.0390625 to 0.0390625
Outputs:
- grad_in: bfloat16 [1024, 8192], P('seq', 'tensor')
- grad_gate: bfloat16 [8192, 24576], P('tensor', 'seq')
- grad_up: bfloat16 [8192, 24576], P('tensor', 'seq')
- grad_down: bfloat16 [24576, 8192], P('seq', 'tensor')
- grad_gain: float32 [8192], P('tensor')
- grad_router: float32 [8192], P('tensor')
The draws below stay inside these ranges and needn't reach their ends.
Inputs may be any that keep to these rules, and one draw needn't show every extreme that they name: `slot_tokens`: slot p belongs to index p // 16 of seq; the live slots of one index hold distinct positions, the others hold arbitrary positions of that index. `live_counts`: in every draw some index of seq has all 16 slots live.
All inputs are finite; a program needn't handle non-finite values.
Results may differ from the reference program's by a relative error of at most 0.0077.
Values may be sent and summed in bfloat16 or wider, within the bound.
No kernel may reach another device: no remote copies, remote signals or barrier semaphores. Data moves between devices by JAX's collectives and lax.ppermute only.
A program may use at most 128 MiB of HBM per device.

```python
import jax
import jax.numpy as jnp
from jax import lax

D = 8192
FF = 24576
TOK_DEV = 128
CAP = 16
TOKENS = 1024
N_SEQ = 8


def routing_draw(key):
    base = jax.random.fold_in(key, 11)
    first, second, third, fourth = jax.random.split(base, 4)
    lowest = max(CAP // 3, 1)
    ranks = jnp.arange(N_SEQ, dtype=jnp.int32)
    floors = lowest + (CAP - lowest) * ranks // max(N_SEQ - 1, 1)
    counts = jax.random.randint(first, (N_SEQ,), floors, CAP + 1, dtype=jnp.int32)
    chosen = jax.random.randint(second, (), 0, N_SEQ, dtype=jnp.int32)
    counts = jnp.where(ranks == chosen, CAP, counts).astype(jnp.int32)
    keys = jax.random.split(third, N_SEQ)
    orders = jax.vmap(lambda single: jax.random.permutation(single, TOK_DEV))(keys)[:, :CAP].astype(jnp.int32)
    filler = jax.random.randint(fourth, (N_SEQ, CAP), 0, TOK_DEV, dtype=jnp.int32)
    columns = jnp.arange(CAP, dtype=jnp.int32)[None, :]
    tokens = jnp.where(columns < counts[:, None], orders, filler).reshape(-1).astype(jnp.int32)
    return (tokens, counts)


def draw_slot_tokens(key, part):
    return routing_draw(key)[0]


def draw_live_counts(key, part):
    return routing_draw(key)[1]


def block_scale(own_key, shape, pieces, least, top_value):
    def one(dim, blocks):
        heights = jax.random.uniform(jax.random.fold_in(jax.random.fold_in(own_key, 6), dim), (blocks,), jnp.float32, least / len(pieces), top_value / len(pieces))
        return jnp.repeat(jnp.exp(heights), shape[dim] // blocks).reshape((-1,) + (1,) * (len(shape) - dim - 1))

    loudness = one(*pieces[0])
    for cut in pieces[1:]:
        loudness = loudness * one(*cut)
    return loudness


def centred(stream_key, extent, spread, bound, cuts=(), kind=jnp.bfloat16):
    array = jax.random.normal(stream_key, extent, jnp.float32) * spread
    if len(cuts) > 0:
        array = block_scale(stream_key, extent, cuts, -0.22, 0.18) * array
    return jnp.clip(array, min=-bound, max=bound).astype(kind)


def setup_inputs(seed: int = 0) -> dict:
    key_list = jax.random.split(jax.random.key(seed), 10)
    return {
        "hidden_in": centred(key_list[0], (TOKENS, D), 1.0, 6.0, ((0, 8), (1, 4))),
        "grad_out": centred(key_list[1], (TOKENS, D), 1.0, 6.0, ((0, 8), (1, 4))),
        "slot_tokens": draw_slot_tokens(jax.random.fold_in(key_list[9], 71), 0),
        "live_counts": draw_live_counts(jax.random.fold_in(key_list[9], 71), 0),
        "norm_gain": jnp.clip(1.0 + 0.1 * jax.random.normal(key_list[4], (D,), jnp.float32), 0.5, 1.5),
        "router_weight": centred(key_list[5], (D,), D ** -0.5, 0.0625, ((0, 4),), jnp.float32),
        "gate_weight": centred(key_list[6], (D, FF), D ** -0.5, 0.0625, ((0, 4), (1, 8))),
        "up_weight": centred(key_list[7], (D, FF), D ** -0.5, 0.0625, ((0, 4), (1, 8))),
        "down_weight": centred(key_list[8], (FF, D), FF ** -0.5, 0.0390625, ((0, 8), (1, 4))),
    }


norm_eps = 1e-06

def silu_parts(gate):
    sig = jax.nn.sigmoid(gate)
    return (gate * sig, sig * (1.0 + gate * (1.0 - sig)))

def reference(hidden_in, grad_out, slot_tokens, live_counts, norm_gain, router_weight, gate_weight, up_weight, down_weight):
    slots = jnp.arange(N_SEQ * CAP, dtype=jnp.int32)
    owners = slots // CAP
    positions = (owners * TOK_DEV + slot_tokens).astype(jnp.int32)
    live_rows = slots % CAP < live_counts[owners]
    picked = jnp.take(hidden_in, positions, axis=0)
    upstream = jnp.where(live_rows[:, None], jnp.take(grad_out, positions, axis=0), jnp.zeros((), jnp.bfloat16))
    wide = picked.astype(jnp.float32)
    inverse = lax.rsqrt(lax.optimization_barrier(jnp.mean(wide * wide, axis=1, keepdims=True)) + norm_eps)
    scaled = wide * inverse
    normed = (scaled * norm_gain).astype(jnp.bfloat16)
    logits = jnp.dot(normed, router_weight.astype(jnp.bfloat16), preferred_element_type=jnp.float32)
    gate = jnp.dot(normed, gate_weight, preferred_element_type=jnp.float32)
    upper = jnp.dot(normed, up_weight, preferred_element_type=jnp.float32)
    back = jnp.dot(upstream, down_weight.T, preferred_element_type=jnp.float32)
    act, slope = silu_parts(gate)
    hidden = act * upper
    weighted = (hidden * logits[:, None]).astype(jnp.bfloat16)
    router_grad = lax.optimization_barrier(jnp.sum(hidden * back, axis=1))
    d_hidden = logits[:, None] * back
    d_gate = (d_hidden * upper * slope).astype(jnp.bfloat16)
    d_up = (d_hidden * act).astype(jnp.bfloat16)
    count_scale = lax.rsqrt(jnp.sum(live_counts).astype(jnp.float32))
    grad_gate = (count_scale * jnp.dot(normed.T, d_gate, preferred_element_type=jnp.float32)).astype(jnp.bfloat16)
    grad_up = (count_scale * jnp.dot(normed.T, d_up, preferred_element_type=jnp.float32)).astype(jnp.bfloat16)
    grad_down = (count_scale * jnp.dot(weighted.T, upstream, preferred_element_type=jnp.float32)).astype(jnp.bfloat16)
    d_normed = jnp.dot(d_gate, gate_weight.T, preferred_element_type=jnp.float32)
    d_normed = d_normed + jnp.dot(d_up, up_weight.T, preferred_element_type=jnp.float32)
    d_normed = d_normed + router_grad[:, None] * router_weight
    grad_gain = count_scale * lax.optimization_barrier(jnp.sum(d_normed * scaled, axis=0))
    grad_router = count_scale * jnp.dot(router_grad, normed.astype(jnp.float32), precision=lax.Precision.HIGHEST)
    d_scaled = d_normed * norm_gain
    d_picked = inverse * (d_scaled - scaled * lax.optimization_barrier(jnp.mean(d_scaled * scaled, axis=1, keepdims=True)))
    d_picked = jnp.where(live_rows[:, None], d_picked, jnp.zeros((), jnp.float32))
    grad_in = grad_out.astype(jnp.float32).at[positions].add(d_picked).astype(jnp.bfloat16)
    return (grad_in, grad_gate, grad_up, grad_down, grad_gain, grad_router)
```

```python
import jax
import jax.numpy as jnp
from jax import lax
from jax.sharding import PartitionSpec as P

norm_eps = 1e-06
f32 = jnp.float32
bf16 = jnp.bfloat16
CHUNKS = 2


def swap(x, axis, bit):
    n = lax.axis_size(axis)
    return lax.ppermute(x, axis, [(i, i ^ bit) for i in range(n)])


def shift(x, step):
    n = lax.axis_size("seq")
    return lax.ppermute(x, "seq", [(i, (i + 2 * step) % n) for i in range(n)])


def butterfly(x, axis):
    bit = 1
    while bit < lax.axis_size(axis):
        x = x + swap(x, axis, bit)
        bit *= 2
    return x


def seq_gather(x):
    ring = lax.axis_size("seq") // 2
    pair = jnp.concatenate([x, swap(x, "seq", 1)], axis=0)
    half = pair.shape[0] // 2
    blocks = [pair]
    up, down = pair, pair
    for k in range(1, ring // 2):
        up, down = shift(up, 1), shift(down, -1)
        blocks += [up, down]
    if ring > 1:
        far_up, far_down = shift(up[:half], 1), shift(down[half:], -1)
        blocks += [far_up, far_down]
    return jnp.concatenate(blocks, axis=0)


def seq_scatter(x):
    n = lax.axis_size("seq")
    ring = n // 2
    rows = x.shape[0] // n
    at = [0]

    def take(count):
        at[0] += count
        return x[at[0] - count : at[0]]

    own = take(2 * rows)
    ups, downs = [], []
    for k in range(1, ring // 2):
        ups.append(take(2 * rows))
        downs.append(take(2 * rows))
    if ring > 1:
        far_up, far_down = take(rows), take(rows)
        acc_d = shift(far_up.astype(bf16), -1).astype(f32)
        acc_u = shift(far_down.astype(bf16), 1).astype(f32)
        pad = jnp.zeros_like(acc_d)
        acc_d = jnp.concatenate([acc_d, pad], axis=0)
        acc_u = jnp.concatenate([pad, acc_u], axis=0)
        for u, d in zip(ups[::-1], downs[::-1]):
            acc_d = shift((u + acc_d).astype(bf16), -1).astype(f32)
            acc_u = shift((d + acc_u).astype(bf16), 1).astype(f32)
        own = own + acc_d + acc_u
    return own[:rows] + swap(own[rows:].astype(bf16), "seq", 1).astype(f32)


def turn(x, flag):
    half = x.shape[0] // 2
    return jnp.where(flag, jnp.concatenate([x[half:], x[:half]], axis=0), x)


def tensor_sum(part):
    half = part.shape[0] // 2
    got = swap(part[half:].astype(bf16), "tensor", 1)
    total = part[:half] + got.astype(f32)
    bit = 2
    while bit < lax.axis_size("tensor"):
        sent = total.astype(bf16)
        total = sent.astype(f32) + swap(sent, "tensor", bit).astype(f32)
        bit *= 2
    return total


def tensor_join(x):
    return jnp.concatenate([x, swap(x, "tensor", 1)], axis=0)


def body(
    hidden_in,
    grad_out,
    slot_tokens,
    live_counts,
    norm_gain,
    router_weight,
    gate_weight,
    up_weight,
    down_weight,
):
    slot_count = slot_tokens.shape[0]
    width_total = hidden_in.shape[1] * lax.axis_size("tensor")
    odd = lax.axis_index("tensor") % 2 == 1
    live_rows = lax.iota(jnp.int32, slot_count) < live_counts[0]
    picked = jnp.take(hidden_in, slot_tokens, axis=0)
    upstream = jnp.where(
        live_rows[:, None], jnp.take(grad_out, slot_tokens, axis=0), jnp.zeros((), bf16)
    )
    count_scale = lax.rsqrt(butterfly(jnp.full((8, 128), live_counts[0], f32), "seq")[0, 0])
    all_upstream = turn(seq_gather(upstream), odd)
    wide = seq_gather(picked).astype(f32)
    inverse = lax.rsqrt(
        butterfly(jnp.sum(wide * wide, axis=1), "tensor") / width_total + norm_eps
    )[:, None]
    scaled = wide * inverse
    normed = (scaled * norm_gain).astype(bf16)
    logit_part = jnp.sum(
        normed.astype(f32) * router_weight.astype(bf16).astype(f32), axis=1
    )
    half = normed.shape[0] // 2
    logits = turn(butterfly(logit_part, "tensor"), odd)[:half, None]
    all_normed = turn(normed, odd)

    hidden_units = gate_weight.shape[1]
    step = hidden_units // CHUNKS
    weighted, d_gate, d_up = [], [], []
    router_grad = jnp.zeros((half,), f32)
    total = jnp.zeros(normed.shape, f32)
    sums = []
    for c in range(CHUNKS):
        cut = slice(c * step, (c + 1) * step)
        back_part = jnp.einsum(
            "pd,fd->pf", all_upstream, down_weight[cut], preferred_element_type=f32
        )
        back = tensor_sum(back_part)
        gate = tensor_sum(jnp.dot(all_normed, gate_weight[:, cut], preferred_element_type=f32))
        upper = tensor_sum(jnp.dot(all_normed, up_weight[:, cut], preferred_element_type=f32))
        sums.append((back, gate, upper))
    for c in range(CHUNKS):
        cut = slice(c * step, (c + 1) * step)
        back, gate, upper = sums[c]
        sig = jax.nn.sigmoid(gate)
        act, slope = gate * sig, sig * (1.0 + gate * (1.0 - sig))
        hidden = act * upper
        router_grad = router_grad + jnp.sum(hidden * back, axis=1)
        d_hidden = logits * back
        dg = tensor_join((d_hidden * upper * slope).astype(bf16))
        du = tensor_join((d_hidden * act).astype(bf16))
        wt = tensor_join((hidden * logits).astype(bf16))
        total = total + jnp.einsum(
            "pf,df->pd", dg, gate_weight[:, cut], preferred_element_type=f32
        )
        total = total + jnp.einsum("pf,df->pd", du, up_weight[:, cut], preferred_element_type=f32)
        weighted.append(wt)
        d_gate.append(dg)
        d_up.append(du)
    router_grad = tensor_join(router_grad)[:, None]
    router_part = jnp.sum(router_grad * all_normed.astype(f32), axis=0)
    total = turn(total + router_grad * router_weight, odd)
    gain_part = jnp.sum(total * scaled, axis=0)
    d_normed = seq_scatter(total)
    small = butterfly(jnp.stack([gain_part, router_part]), "seq")

    own_scaled = scaled[:slot_count]
    d_scaled = d_normed * norm_gain
    inner = butterfly(jnp.sum(d_scaled * own_scaled, axis=1), "tensor") / width_total
    d_picked = inverse[:slot_count] * (d_scaled - own_scaled * inner[:, None])
    d_picked = jnp.where(live_rows[:, None], d_picked, jnp.zeros((), f32))
    spots = (
        lax.broadcasted_iota(jnp.int32, (grad_out.shape[0], slot_count), 0) == slot_tokens[None, :]
    ).astype(f32)
    placed = jnp.dot(spots, d_picked, precision=lax.Precision.HIGHEST)
    grad_in = (grad_out.astype(f32) + placed).astype(bf16)

    weighted, d_gate, d_up = (jnp.concatenate(v, axis=1) for v in (weighted, d_gate, d_up))
    grad_gate = jnp.einsum("pd,pf->df", all_normed, d_gate, preferred_element_type=f32)
    grad_up = jnp.einsum("pd,pf->df", all_normed, d_up, preferred_element_type=f32)
    grad_down = jnp.einsum("pf,pd->fd", weighted, all_upstream, preferred_element_type=f32)
    return (
        grad_in,
        (count_scale * grad_gate).astype(bf16),
        (count_scale * grad_up).astype(bf16),
        (count_scale * grad_down).astype(bf16),
        count_scale * small[0],
        count_scale * small[1],
    )


def solution(mesh):
    in_specs = (
        P("seq", "tensor"),
        P("seq", "tensor"),
        P("seq"),
        P("seq"),
        P("tensor"),
        P("tensor"),
        P("tensor", "seq"),
        P("tensor", "seq"),
        P("seq", "tensor"),
    )
    out_specs = (
        P("seq", "tensor"),
        P("tensor", "seq"),
        P("tensor", "seq"),
        P("seq", "tensor"),
        P("tensor"),
        P("tensor"),
    )
    return jax.shard_map(body, mesh=mesh, in_specs=in_specs, out_specs=out_specs, check_vma=False)
```

```python
import jax
import jax.numpy as jnp
from jax import lax
from jax.sharding import PartitionSpec as P

norm_eps = 1e-06
f32 = jnp.float32
bf16 = jnp.bfloat16
CHUNKS = 2


def swap(x, axis, bit):
    n = lax.axis_size(axis)
    return lax.ppermute(x, axis, [(i, i ^ bit) for i in range(n)])


def shift(x, step):
    n = lax.axis_size("seq")
    return lax.ppermute(x, "seq", [(i, (i + 2 * step) % n) for i in range(n)])


def butterfly(x, axis):
    bit = 1
    while bit < lax.axis_size(axis):
        x = x + swap(x, axis, bit)
        bit *= 2
    return x


def seq_gather(x):
    ring = lax.axis_size("seq") // 2
    pair = jnp.concatenate([x, swap(x, "seq", 1)], axis=0)
    half = pair.shape[0] // 2
    blocks = [pair]
    up, down = pair, pair
    for k in range(1, ring // 2):
        up, down = shift(up, 1), shift(down, -1)
        blocks += [up, down]
    if ring > 1:
        far_up, far_down = shift(up[:half], 1), shift(down[half:], -1)
        blocks += [far_up, far_down]
    return jnp.concatenate(blocks, axis=0)


def seq_scatter(x, tie):
    n = lax.axis_size("seq")
    ring = n // 2
    rows = x.shape[0] // n
    at = [0]

    def take(count):
        at[0] += count
        return x[at[0] - count : at[0]]

    own = take(2 * rows)
    ups, downs = [], []
    for k in range(1, ring // 2):
        ups.append(take(2 * rows))
        downs.append(take(2 * rows))
    if ring > 1:
        far_up, far_down = take(rows), take(rows)
        acc_d = shift(far_up.astype(bf16), -1).astype(f32)
        acc_u = shift(far_down.astype(bf16), 1).astype(f32)
        acc_d, acc_u = tie(acc_d, acc_u)
        pad = jnp.zeros_like(acc_d)
        acc_d = jnp.concatenate([acc_d, pad], axis=0)
        acc_u = jnp.concatenate([pad, acc_u], axis=0)
        for u, d in zip(ups[::-1], downs[::-1]):
            acc_d = shift((u + acc_d).astype(bf16), -1).astype(f32)
            acc_u = shift((d + acc_u).astype(bf16), 1).astype(f32)
            acc_d, acc_u = tie(acc_d, acc_u)
        own = own + acc_d + acc_u
    return own[:rows] + swap(own[rows:].astype(bf16), "seq", 1).astype(f32)


def turn(x, flag):
    half = x.shape[0] // 2
    return jnp.where(flag, jnp.concatenate([x[half:], x[:half]], axis=0), x)


def tensor_sum(part):
    half = part.shape[0] // 2
    return tensor_rest(part[:half], swap(part[half:].astype(bf16), "tensor", 1))


def tensor_rest(own, got):
    total = own + got.astype(f32)
    bit = 2
    while bit < lax.axis_size("tensor"):
        sent = total.astype(bf16)
        total = sent.astype(f32) + swap(sent, "tensor", bit).astype(f32)
        bit *= 2
    return total


def tensor_join(x):
    return jnp.concatenate([x, swap(x, "tensor", 1)], axis=0)


def body(
    hidden_in,
    grad_out,
    slot_tokens,
    live_counts,
    norm_gain,
    router_weight,
    gate_weight,
    up_weight,
    down_weight,
):
    slot_count = slot_tokens.shape[0]
    width_total = hidden_in.shape[1] * lax.axis_size("tensor")
    odd = lax.axis_index("tensor") % 2 == 1
    live_rows = lax.iota(jnp.int32, slot_count) < live_counts[0]
    picked = jnp.take(hidden_in, slot_tokens, axis=0)
    upstream = jnp.where(
        live_rows[:, None], jnp.take(grad_out, slot_tokens, axis=0), jnp.zeros((), bf16)
    )
    count_scale = lax.rsqrt(butterfly(jnp.full((8, 128), live_counts[0], f32), "seq")[0, 0])
    all_upstream = turn(seq_gather(upstream), odd)
    wide = seq_gather(picked).astype(f32)
    inverse = lax.rsqrt(
        butterfly(jnp.sum(wide * wide, axis=1), "tensor") / width_total + norm_eps
    )[:, None]
    scaled = wide * inverse
    normed = (scaled * norm_gain).astype(bf16)
    logit_part = jnp.sum(
        normed.astype(f32) * router_weight.astype(bf16).astype(f32), axis=1
    )
    half = normed.shape[0] // 2
    logits = turn(butterfly(logit_part, "tensor"), odd)[:half, None]
    all_normed = turn(normed, odd)

    hidden_units = gate_weight.shape[1]
    step = hidden_units // CHUNKS
    weighted, d_gate, d_up = [], [], []
    router_grad = jnp.zeros((half,), f32)
    total = jnp.zeros(normed.shape, f32)
    sums = []
    backs = []
    for c in range(CHUNKS):
        back_part = jnp.einsum(
            "pd,fd->pf",
            all_upstream,
            down_weight[c * step : (c + 1) * step],
            preferred_element_type=f32,
        )
        got = swap(back_part[half:].astype(bf16), "tensor", 1)
        all_normed, got = lax.optimization_barrier((all_normed, got))
        backs.append(tensor_rest(back_part[:half], got))
    for c in range(CHUNKS):
        cut = slice(c * step, (c + 1) * step)
        back = backs[c]
        gate = tensor_sum(jnp.dot(all_normed, gate_weight[:, cut], preferred_element_type=f32))
        upper = tensor_sum(jnp.dot(all_normed, up_weight[:, cut], preferred_element_type=f32))
        sums.append((back, gate, upper))
    for c in range(CHUNKS):
        cut = slice(c * step, (c + 1) * step)
        back, gate, upper = sums[c]
        sig = jax.nn.sigmoid(gate)
        act, slope = gate * sig, sig * (1.0 + gate * (1.0 - sig))
        hidden = act * upper
        router_grad = router_grad + jnp.sum(hidden * back, axis=1)
        d_hidden = logits * back
        dg = tensor_join((d_hidden * upper * slope).astype(bf16))
        du = tensor_join((d_hidden * act).astype(bf16))
        wt = tensor_join((hidden * logits).astype(bf16))
        total = total + jnp.einsum(
            "pf,df->pd", dg, gate_weight[:, cut], preferred_element_type=f32
        )
        total = total + jnp.einsum("pf,df->pd", du, up_weight[:, cut], preferred_element_type=f32)
        weighted.append(wt)
        d_gate.append(dg)
        d_up.append(du)
    router_grad = tensor_join(router_grad)[:, None]
    router_part = jnp.sum(router_grad * all_normed.astype(f32), axis=0)
    total = turn(total + router_grad * router_weight, odd)
    gain_part = jnp.sum(total * scaled, axis=0)
    weighted, d_gate, d_up = (jnp.concatenate(v, axis=1) for v in (weighted, d_gate, d_up))
    held = [d_gate, d_up]
    at = [0, 1]
    small = [jnp.stack([gain_part, router_part])]

    def tie(*sums):
        if at[0] == len(held):
            return sums
        if at[1] < lax.axis_size("seq"):
            small[0] = small[0] + swap(small[0], "seq", at[1])
            at[1] *= 2
        held[at[0]], small[0], *sums = lax.optimization_barrier((held[at[0]], small[0], *sums))
        at[0] += 1
        return sums

    d_normed = seq_scatter(total, tie)
    d_gate, d_up = held
    small = small[0]
    while at[1] < lax.axis_size("seq"):
        small = small + swap(small, "seq", at[1])
        at[1] *= 2

    own_scaled = scaled[:slot_count]
    d_scaled = d_normed * norm_gain
    inner = butterfly(jnp.sum(d_scaled * own_scaled, axis=1), "tensor") / width_total
    d_picked = inverse[:slot_count] * (d_scaled - own_scaled * inner[:, None])
    d_picked = jnp.where(live_rows[:, None], d_picked, jnp.zeros((), f32))
    spots = (
        lax.broadcasted_iota(jnp.int32, (grad_out.shape[0], slot_count), 0) == slot_tokens[None, :]
    ).astype(f32)
    placed = jnp.dot(spots, d_picked, precision=lax.Precision.HIGHEST)
    grad_in = (grad_out.astype(f32) + placed).astype(bf16)

    grad_gate = jnp.einsum("pd,pf->df", all_normed, d_gate, preferred_element_type=f32)
    grad_up = jnp.einsum("pd,pf->df", all_normed, d_up, preferred_element_type=f32)
    grad_down = jnp.einsum("pf,pd->fd", weighted, all_upstream, preferred_element_type=f32)
    return (
        grad_in,
        (count_scale * grad_gate).astype(bf16),
        (count_scale * grad_up).astype(bf16),
        (count_scale * grad_down).astype(bf16),
        count_scale * small[0],
        count_scale * small[1],
    )


def solution(mesh):
    in_specs = (
        P("seq", "tensor"),
        P("seq", "tensor"),
        P("seq"),
        P("seq"),
        P("tensor"),
        P("tensor"),
        P("tensor", "seq"),
        P("tensor", "seq"),
        P("seq", "tensor"),
    )
    out_specs = (
        P("seq", "tensor"),
        P("tensor", "seq"),
        P("tensor", "seq"),
        P("seq", "tensor"),
        P("tensor"),
        P("tensor"),
    )
    return jax.shard_map(body, mesh=mesh, in_specs=in_specs, out_specs=out_specs, check_vma=False)
```
